1024 devices in a mesh: seq: 128 (over y, z), head: 8 (over x, core).
Axes of the slice: x: 4, y: 4, z: 32, core: 2. Of those that a mesh axis runs over, the one named last changes fastest.
Arguments:
- queries: bfloat16 [16384, 3072], P('seq', 'head'), may hold values from -2 to 2
- key_rows: bfloat16 [16384, 3072], P('seq', 'head'), may hold values from -2 to 2
- values: bfloat16 [16384, 3072], P('seq', 'head'), may hold values from -6 to 6
- conv_input: bfloat16 [16384, 3072], P('seq', 'head'), may hold values from -0.14941406 to 0.14941406
- log_gates: bfloat16 [16384, 3072], P('seq', 'head'), may hold values from -1 to 0
- grad_output: bfloat16 [16384, 3072], P('seq', 'head'), may hold values from -0.8984375 to 0.8984375
- saved_state: float32 [128, 24, 128, 128], P('seq', 'head'), may hold values from -6 to 6
- conv_kernel: float32 [4, 3072], replicated, may hold values from -3 to 3
Outputs:
- grad_queries: bfloat16 [16384, 3072], P('seq', 'head')
- grad_keys: bfloat16 [16384, 3072], P('seq', 'head')
- grad_gates: bfloat16 [16384, 3072], P('seq', 'head')
- grad_input: bfloat16 [16384, 3072], P(('seq', 'head'))
- grad_kernel: float32 [4, 3072], P(None, 'head')
The draws below stay inside these ranges and needn't reach their ends.
All inputs are finite; a program needn't handle non-finite values.
Results may differ from the reference program's by a relative error of at most 0.0049.
Values may be sent and summed in bfloat16 or wider, within the bound.
No kernel may reach another device: no remote copies, remote signals or barrier semaphores. Data moves between devices by JAX's collectives and lax.ppermute only.
A program may use at most 64 MiB of HBM per device.

```python
import math
import jax
import jax.numpy as jnp
from jax import lax

HEADS = 24
DK = 128
DV = 128
STRETCH = 64
KW = 4
TOK_DEV = 128
SPAN_POSITIONS = 16384
BLOCKS = 128


def channel_rates(key):
    pick_key, slow_key, fast_key = jax.random.split(jax.random.fold_in(key, 7), 3)
    width = HEADS * DK
    share = 0.5
    fast = jax.random.uniform(pick_key, (width,)) < share
    slow_rate = jnp.exp(jax.random.uniform(slow_key, (width,), minval=math.log(0.05), maxval=math.log(0.5))) / SPAN_POSITIONS
    quick_decay_rate = jnp.exp(jax.random.uniform(fast_key, (width,), minval=math.log(1.0 / 50.0), maxval=math.log(1.0 / 30.0)))
    return jnp.where(fast, quick_decay_rate, slow_rate)


def scaled_rows(key, salt):
    fading_speeds = channel_rates(key)
    noise_key = jax.random.fold_in(jax.random.fold_in(key, salt), 0)
    shape = (SPAN_POSITIONS, HEADS * DK)
    noise = jnp.clip(jax.random.normal(noise_key, shape), -6.0, 6.0)
    return (noise * jnp.sqrt(2.0 * fading_speeds)[None, :]).astype(jnp.bfloat16)


def draw_queries(key, part):
    return scaled_rows(key, 21)


def draw_key_rows(key, part):
    return scaled_rows(key, 22)


def draw_log_gates(key, part):
    fading_speeds = channel_rates(key)
    width = HEADS * DK
    blocks = SPAN_POSITIONS // TOK_DEV
    mod_key, rough_key, place_key, loss_key = jax.random.split(jax.random.fold_in(key, 11), 4)
    scaling_multiplier = jnp.repeat(jnp.exp(jax.random.uniform(mod_key, (blocks, width), minval=-0.7, maxval=0.7)), TOK_DEV, axis=0)
    coarse_perturbation = jnp.exp(jax.random.uniform(rough_key, (SPAN_POSITIONS, width), minval=math.log(0.5), maxval=math.log(1.5)))
    position_offsets = jax.random.randint(place_key, (3,), 0, SPAN_POSITIONS)
    spike_amplitudes = jnp.any(jnp.arange(SPAN_POSITIONS)[:, None] == position_offsets[None, :], axis=1)
    objective_scores = jnp.log(jax.random.uniform(loss_key, (SPAN_POSITIONS, width), minval=0.6, maxval=0.8))
    forgetting_levels = -fading_speeds[None, :] * coarse_perturbation * scaling_multiplier + jnp.where(spike_amplitudes[:, None], objective_scores, 0.0)
    return forgetting_levels.astype(jnp.bfloat16)


def level_of(key, shape, pieces, smallest, top_value):
    loudness, own = 1.0, jax.random.fold_in(key, 6)
    for axis_at, parts in pieces:
        heights = jnp.exp(jax.random.uniform(jax.random.fold_in(own, axis_at), (parts,), jnp.float32, smallest / len(pieces), top_value / len(pieces)))
        loudness = loudness * jnp.repeat(heights, shape[axis_at] // parts).reshape([-1 if axis == axis_at else 1 for axis in range(len(shape))])
    return loudness


def bell_draw(rng, extent, scale, limit, pieces=(), dtype=jnp.bfloat16):
    entries = scale * jax.random.normal(rng, extent, jnp.float32)
    if pieces:
        entries = entries * level_of(rng, extent, pieces, -0.22, 0.18)
    return jnp.clip(entries, -limit, limit).astype(dtype)


def setup_inputs(seed: int = 0) -> dict:
    key_list = jax.random.split(jax.random.key(seed), 9)
    return {
        "queries": draw_queries(jax.random.fold_in(key_list[8], 71), 0),
        "key_rows": draw_key_rows(jax.random.fold_in(key_list[8], 71), 0),
        "values": bell_draw(key_list[2], (SPAN_POSITIONS, HEADS * DV), 1.0, 6.0, ((0, 128), (1, 8))),
        "conv_input": bell_draw(key_list[3], (SPAN_POSITIONS, HEADS * DV), 0.025, 0.14941406, ((0, 128), (1, 8))),
        "log_gates": draw_log_gates(jax.random.fold_in(key_list[8], 71), 0),
        "grad_output": bell_draw(key_list[5], (SPAN_POSITIONS, HEADS * DV), 0.15, 0.8984375, ((0, 128), (1, 8))),
        "saved_state": bell_draw(key_list[6], (BLOCKS, HEADS, DK, DV), 1.0, 6.0, ((0, 128), (1, 8)), jnp.float32),
        "conv_kernel": bell_draw(key_list[7], (KW, HEADS * DV), 0.5, 3.0, (), jnp.float32),
    }


PRECISE = lax.Precision.HIGHEST

def shard_pass(queries, key_rows, values, log_gates, grad_out, start_state, incoming):
    length = queries.shape[0]
    stretches = length // STRETCH
    query_c = queries.reshape((stretches, STRETCH) + queries.shape[1:])
    key_c = key_rows.reshape((stretches, STRETCH) + key_rows.shape[1:])
    value_c = values.reshape((stretches, STRETCH) + values.shape[1:])
    grad_c = grad_out.reshape((stretches, STRETCH) + grad_out.shape[1:])
    within = jnp.cumsum(log_gates.reshape((stretches, STRETCH) + log_gates.shape[1:]), axis=1)
    running_totals = within[:, -1]
    query_up = query_c * jnp.exp(within)
    key_down = key_c * jnp.exp(-within)
    key_tail = key_c * jnp.exp(running_totals[:, None] - within)
    growth = jnp.einsum('ntha,nthe->nhae', key_tail, value_c, precision=PRECISE)

    def step_forward(current, inputs):
        decays, addend = inputs
        return (jnp.exp(decays)[..., None] * current + addend, current)
    last_state, starts = lax.scan(step_forward, start_state, (running_totals, growth))
    pushes = jnp.einsum('ntha,nthe->nhae', query_up, grad_c, precision=PRECISE)
    leaving, stretch_ends = lax.scan(step_forward, incoming, (running_totals, pushes), reverse=True)
    steps_idx = jnp.arange(STRETCH)
    lower_mask = (steps_idx[:, None] >= steps_idx[None, :]).astype(jnp.float32)
    scores = jnp.einsum('nthe,nshe->nhts', grad_c, value_c, precision=PRECISE) * lower_mask
    grad_query = jnp.exp(within) * (jnp.einsum('nthe,nhae->ntha', grad_c, starts, precision=PRECISE) + jnp.einsum('nhts,nsha->ntha', scores, key_down, precision=PRECISE))
    grad_key = jnp.exp(-within) * jnp.einsum('nhts,ntha->nsha', scores, query_up, precision=PRECISE) + jnp.exp(running_totals[:, None] - within) * jnp.einsum('nshe,nhae->nsha', value_c, stretch_ends, precision=PRECISE)
    weights = jnp.einsum('nsha,ntha->nhst', key_down, query_up, precision=PRECISE) * lower_mask.T
    grad_value = jnp.einsum('nhst,nthe->nshe', weights, grad_c, precision=PRECISE) + jnp.einsum('nsha,nhae->nshe', key_tail, stretch_ends, precision=PRECISE)
    return (grad_query.reshape(queries.shape), grad_key.reshape(key_rows.shape), grad_value.reshape(values.shape), last_state, leaving)

def gate_grad(queries, grad_query, key_rows, grad_key, incoming, last_state):
    terms = queries * grad_query - key_rows * grad_key
    backward_sum = jnp.cumsum(terms[::-1], axis=0)[::-1]
    return backward_sum + lax.optimization_barrier(jnp.sum(incoming * last_state, axis=-1))[None]

def reference(queries, key_rows, values, conv_input, log_gates, grad_output, saved_state, conv_kernel):
    columns = HEADS * DV

    def blocked(array, width):
        return array.reshape(BLOCKS, TOK_DEV, HEADS, width)

    def step(running, inputs):
        incoming, next_rows, kernel_accumulated_sum = running
        query_b, key_b, value_b, input_b, gate_b, grad_b, start_b = inputs
        query_f = query_b.astype(jnp.float32)
        key_f = key_b.astype(jnp.float32)
        grad_query, grad_key, grad_value, last_state, leaving = shard_pass(query_f, key_f, value_b.astype(jnp.float32), gate_b.astype(jnp.float32), grad_b.astype(jnp.float32), start_b, incoming)
        grad_gate = gate_grad(query_f, grad_query, key_f, grad_key, incoming, last_state)
        rounded = lax.optimization_barrier(grad_value.reshape(TOK_DEV, columns).astype(jnp.bfloat16)).astype(jnp.float32)
        padded = jnp.concatenate([rounded, next_rows], axis=0)
        input_f = input_b.astype(jnp.float32)
        conv_grad = jnp.zeros((TOK_DEV, columns), jnp.float32)
        tap_terms = []
        for tap_index in range(KW):
            window = padded[tap_index:tap_index + TOK_DEV]
            conv_grad = conv_grad + conv_kernel[tap_index] * window
            tap_terms.append(lax.optimization_barrier(jnp.sum(input_f * window, axis=0)))
        outputs = (grad_query.reshape(TOK_DEV, HEADS * DK).astype(jnp.bfloat16), grad_key.reshape(TOK_DEV, HEADS * DK).astype(jnp.bfloat16), grad_gate.reshape(TOK_DEV, HEADS * DK).astype(jnp.bfloat16), conv_grad.astype(jnp.bfloat16))
        return ((leaving, rounded[:KW - 1], kernel_accumulated_sum + jnp.stack(tap_terms)), outputs)
    initial = (jnp.zeros((HEADS, DK, DV), jnp.float32), jnp.zeros((KW - 1, columns), jnp.float32), jnp.zeros((KW, columns), jnp.float32))
    inputs = (blocked(queries, DK), blocked(key_rows, DK), blocked(values, DV), conv_input.reshape(BLOCKS, TOK_DEV, columns), blocked(log_gates, DK), blocked(grad_output, DV), saved_state)
    final, stacked = lax.scan(step, initial, inputs, reverse=True)
    grad_queries = stacked[0].reshape(SPAN_POSITIONS, HEADS * DK)
    grad_keys = stacked[1].reshape(SPAN_POSITIONS, HEADS * DK)
    grad_gates = stacked[2].reshape(SPAN_POSITIONS, HEADS * DK)
    grad_input = stacked[3].reshape(SPAN_POSITIONS, columns)
    return (grad_queries, grad_keys, grad_gates, grad_input, final[2])
```

```python
import jax
import jax.numpy as jnp
from jax import lax
from jax.sharding import Mesh, PartitionSpec as P

DK = 128
DV = 128
STRETCH = 64


PRECISE = lax.Precision.HIGHEST


SEQ = ("y", "zh", "zl")
HEAD = ("x", "core")


def exchange(x, axis):
    return lax.all_to_all(x, axis, 0, 0, tiled=True)


def later_blocks(log_decay, push):
    head_count, dk, dv = push.shape
    count = lax.axis_size(SEQ)
    rows = head_count * dk // count
    logs = log_decay.reshape(count, rows)
    high = lax.reduce_precision(logs, 8, 7)
    low = logs - high
    tail = jnp.concatenate([high, low], axis=1)
    tail = jnp.pad(tail, ((0, 0), (0, dv - 2 * rows)))[:, None]
    sent = jnp.concatenate([push.reshape(count, rows, dv), tail], axis=1).astype(jnp.bfloat16)
    got = exchange(sent, SEQ).astype(jnp.float32)
    logs = (got[:, rows, :rows] + got[:, rows, rows : 2 * rows]).T
    at = jnp.arange(count)
    totals = jnp.einsum("rb,bc->rc", logs, (at[:, None] <= at[None, :]).astype(jnp.float32), precision=PRECISE)
    before = totals - logs
    gap = before[:, None, :] - totals[:, :, None]
    weight = jnp.where(at[:, None] < at[None, :], jnp.exp(jnp.minimum(gap, 0.0)), 0.0)
    ended = jnp.einsum("rbc,cre->bre", weight, got[:, :rows], precision=PRECISE)
    back = exchange(ended.astype(jnp.bfloat16), SEQ)
    return back.astype(jnp.float32).reshape(head_count, dk, dv)


def sum_all(x):
    for axis in (("y", "zl"), "zh"):
        every = jnp.broadcast_to(x[None], (lax.axis_size(axis),) + x.shape)
        x = jnp.sum(exchange(every, axis), axis=0)
    return x


def passed_along(x, axis, by):
    count = lax.axis_size(axis)
    pairs = [(i, i + by) for i in range(count) if 0 <= i + by < count]
    return lax.ppermute(x, axis, pairs)


def to_heads(array, head_count, width):
    length = array.shape[0]
    turned = array.reshape(length, head_count, width).transpose(1, 0, 2).astype(jnp.float32)
    return turned.reshape(head_count, length // STRETCH, STRETCH, width)


def from_heads(array):
    head_count, stretches, span, width = array.shape
    return (
        array.reshape(head_count, stretches * span, width)
        .transpose(1, 0, 2)
        .reshape(stretches * span, head_count * width)
    )


def linked_sequence(running_totals, summand_terms, beginning_position, backward_sweep):

    def step_forward(current, inputs):
        decays, addend = inputs
        return (jnp.exp(decays)[..., None] * current + addend, current)

    final, visited = lax.scan(
        step_forward,
        beginning_position,
        (jnp.moveaxis(running_totals, 1, 0), jnp.moveaxis(summand_terms, 1, 0)),
        reverse=backward_sweep,
    )
    return (final, jnp.moveaxis(visited, 0, 1))


def local_grads(
    grad_c, value_c, within, running_totals, query_up, key_down, key_tail, starts, ends
):
    steps_idx = jnp.arange(STRETCH)
    lower_mask = (steps_idx[:, None] >= steps_idx[None, :]).astype(jnp.float32)
    scores = jnp.einsum("hnte,hnse->hnts", grad_c, value_c, precision=PRECISE) * lower_mask
    grad_query = jnp.exp(within) * (
        jnp.einsum("hnte,hnae->hnta", grad_c, starts, precision=PRECISE)
        + jnp.einsum("hnts,hnsa->hnta", scores, key_down, precision=PRECISE)
    )
    grad_key = jnp.exp(-within) * jnp.einsum(
        "hnts,hnta->hnsa", scores, query_up, precision=PRECISE
    ) + jnp.exp(running_totals[:, :, None] - within) * jnp.einsum(
        "hnse,hnae->hnsa", value_c, ends, precision=PRECISE
    )
    weights = jnp.einsum("hnsa,hnta->hnst", key_down, query_up, precision=PRECISE) * lower_mask.T
    grad_value = jnp.einsum("hnst,hnte->hnse", weights, grad_c, precision=PRECISE) + jnp.einsum(
        "hnsa,hnae->hnse", key_tail, ends, precision=PRECISE
    )
    return (grad_query, grad_key, grad_value)


def per_device(
    queries, key_rows, values, conv_input, log_gates, grad_output, saved_state, conv_kernel
):
    length = queries.shape[0]
    head_count = saved_state.shape[1]
    columns = head_count * DV
    tap_count = conv_kernel.shape[0]
    query_c = to_heads(queries, head_count, DK)
    key_c = to_heads(key_rows, head_count, DK)
    value_c = to_heads(values, head_count, DV)
    gate_c = to_heads(log_gates, head_count, DK)
    grad_c = to_heads(grad_output, head_count, DV)
    within = jnp.cumsum(gate_c, axis=2)
    running_totals = within[:, :, -1]
    query_up = query_c * jnp.exp(within)
    key_down = key_c * jnp.exp(-within)
    tail = jnp.exp(running_totals[:, :, None] - within)
    key_tail = key_c * tail
    growth = jnp.einsum("hnta,hnte->hnae", key_tail, value_c, precision=PRECISE)
    pushes = jnp.einsum("hnta,hnte->hnae", query_up, grad_c, precision=PRECISE)
    last_state, starts = linked_sequence(running_totals, growth, saved_state[0], False)
    zero_state = jnp.zeros((head_count, DK, DV), jnp.float32)
    shard_push, ends_alone = linked_sequence(running_totals, pushes, zero_state, True)
    all_decay = jnp.sum(running_totals, axis=1)
    incoming = later_blocks(all_decay, shard_push)
    leaving, ends = linked_sequence(running_totals, pushes, incoming, True)
    grad_query, grad_key, grad_value = local_grads(
        grad_c, value_c, within, running_totals, query_up, key_down, key_tail, starts, ends
    )
    terms = query_c * grad_query - key_c * grad_key
    steps_idx = jnp.arange(STRETCH)
    upper_mask = (steps_idx[:, None] <= steps_idx[None, :]).astype(jnp.float32)
    inside = jnp.einsum("ts,hnsa->hnta", upper_mask, terms, precision=PRECISE)
    stretch_sums = jnp.sum(terms, axis=2)
    after = jnp.sum(stretch_sums, axis=1)[:, None] - jnp.cumsum(stretch_sums, axis=1)
    own_term = jnp.sum(incoming * last_state, axis=-1)
    grad_gate = inside + after[:, :, None] + own_term[:, None, None]
    grad_rows = from_heads(grad_value).astype(jnp.bfloat16)
    kernel_part = lax.dynamic_slice_in_dim(
        conv_kernel, lax.axis_index(HEAD) * columns, columns, 1
    )
    before_rows = passed_along(conv_input[1 - tap_count :], SEQ, 1)
    input_f = jnp.concatenate([before_rows, conv_input], axis=0).astype(jnp.float32)
    next_rows = passed_along(grad_rows[: tap_count - 1], SEQ, -1)
    padded = jnp.concatenate([grad_rows, next_rows], axis=0).astype(jnp.float32)
    own_rows = grad_rows.astype(jnp.float32)
    conv_grad = jnp.zeros((length, columns), jnp.float32)
    tap_terms = []
    for tap_index in range(tap_count):
        conv_grad = conv_grad + kernel_part[tap_index] * padded[tap_index : tap_index + length]
        start = tap_count - 1 - tap_index
        tap_terms.append(jnp.sum(input_f[start : start + length] * own_rows, axis=0))
    grad_kernel = sum_all(jnp.stack(tap_terms))
    grad_input = lax.all_to_all(
        conv_grad.astype(jnp.bfloat16), HEAD, split_axis=0, concat_axis=1, tiled=True
    )
    grad_queries = from_heads(grad_query).astype(jnp.bfloat16)
    grad_keys = from_heads(grad_key).astype(jnp.bfloat16)
    grad_gates = from_heads(grad_gate).astype(jnp.bfloat16)
    return (grad_queries, grad_keys, grad_gates, grad_input, grad_kernel)


def solution(mesh):
    fine = Mesh(mesh.devices.reshape(4, 8, 4, 4, 2), SEQ + HEAD)
    rows = P(SEQ, HEAD)
    return jax.shard_map(
        per_device,
        mesh=fine,
        in_specs=(rows, rows, rows, rows, rows, rows, P(SEQ, HEAD, None, None), P()),
        out_specs=(rows, rows, rows, P(SEQ + HEAD, None), P(None, HEAD)),
        check_vma=False,
    )
```

```python
import jax
import jax.numpy as jnp
from jax import lax
from jax.experimental import pallas as pl
from jax.experimental.pallas import tpu as pltpu
from jax.sharding import Mesh, PartitionSpec as P

HEADS = 3
WIDTH = 128
LEN = 128
STRETCH = 64
TAPS = 4
NEAR = 16
FAR = 8
PEERS = 8
ROWS = 32
SEQ = ("y", "zh", "zl")
HEAD = ("x", "core")
GROUP = ("y", "zl")
F32 = jnp.float32
BF16 = jnp.bfloat16
PRECISE = lax.Precision.HIGHEST


def dot(a, b, over_a=1, over_b=0, precision=None):
    return lax.dot_general(
        a, b, (((over_a,), (over_b,)), ((), ())), precision=precision, preferred_element_type=F32
    )


def dot_exact(a, b, over_a=1, over_b=0):
    return dot(a.astype(F32), b.astype(F32), over_a, over_b, PRECISE)


def two_parts(a):
    high = a.astype(BF16)
    return high, (a - high.astype(F32)).astype(BF16)


def dot_left(a, b, over_a=1, over_b=0):
    high, low = two_parts(a)
    return dot(high, b, over_a, over_b) + dot(low, b, over_a, over_b)


def dot_right(a, b, over_a=1, over_b=0):
    high, low = two_parts(b)
    return dot(a, high, over_a, over_b) + dot(a, low, over_a, over_b)


def ordered(size, compare):
    row = lax.broadcasted_iota(jnp.int32, (size, size), 0)
    column = lax.broadcasted_iota(jnp.int32, (size, size), 1)
    return compare(row, column)


def head_of(x, h):
    return x[:, h * WIDTH : (h + 1) * WIDTH]


def tail_rows(logs):
    row = lax.broadcasted_iota(jnp.int32, (8, WIDTH), 0)
    tail = jnp.zeros((8, WIDTH), F32)
    for h in range(HEADS):
        high = logs[h].astype(BF16).astype(F32)
        low = logs[h] - high
        tail = jnp.where(row == h, high, tail)
        tail = jnp.where(row == HEADS + h, low, tail)
    return tail


def push_of(queries, log_gates, grad_output):
    lower = ordered(LEN, lambda r, c: r >= c).astype(F32).astype(BF16)
    within = dot(lower, log_gates)
    query_up = queries.astype(F32) * jnp.exp(within)
    pushes = [
        dot_left(head_of(query_up, h), head_of(grad_output, h), 0, 0).reshape(NEAR, 8, WIDTH)
        for h in range(HEADS)
    ]
    last = within[LEN - 1 : LEN]
    tail = tail_rows([head_of(last, h) for h in range(HEADS)])
    tail = jnp.broadcast_to(tail[None], (NEAR, 8, WIDTH))
    return jnp.concatenate(pushes + [tail], axis=1).astype(BF16)


def logs_of(tail):
    return [tail[h : h + 1] + tail[HEADS + h : HEADS + h + 1] for h in range(HEADS)]


def decays_of(logs, place):
    lane = lax.broadcasted_iota(jnp.int32, (8, WIDTH), 1)
    row = lax.broadcasted_iota(jnp.int32, (8, WIDTH), 0)
    mine = lane == row + 8 * place
    picked = [jnp.sum(jnp.where(mine, logs[h], 0.0), axis=1, keepdims=True) for h in range(HEADS)]
    return jnp.concatenate([jnp.broadcast_to(jnp.exp(p), (8, WIDTH)) for p in picked], axis=0)


def run_of(got, place):
    x = got.astype(F32)
    logs = logs_of(x[8 * HEADS :])
    return x[: 8 * HEADS], decays_of(logs, place), logs


def group_of(got, place):
    runs = []
    for y in range(4):
        running = jnp.zeros((8 * HEADS, WIDTH), F32)
        total = [jnp.zeros((1, WIDTH), F32)] * HEADS
        for zl in (3, 2, 1, 0):
            push, decay, logs = run_of(got[y * 4 + zl], place)
            running = push + decay * running
            total = [a + b for a, b in zip(total, logs)]
        runs.append(jnp.concatenate([running, tail_rows(total)], axis=0).astype(BF16))
    return runs


def ends_of(near, far, place, mine):
    ends = [None] * NEAR
    running = jnp.zeros((8 * HEADS, WIDTH), F32)
    for y in (3, 2, 1, 0):
        entering = jnp.zeros((8 * HEADS, WIDTH), F32)
        for zh in range(FAR - 1, -1, -1):
            entering = jnp.where(mine == zh, running, entering)
            push, decay, _ = run_of(far[zh, y], place)
            running = push + decay * running
        for zl in (3, 2, 1, 0):
            ends[y * 4 + zl] = entering.astype(BF16)
            push, decay, _ = run_of(near[y * 4 + zl], place)
            entering = push + decay * entering
    return ends


def local_of(queries, key_rows, values, log_gates, grad_output, start):
    q, k = queries.astype(F32), key_rows.astype(F32)
    lower = ordered(STRETCH, lambda r, c: r >= c)
    stretches = []
    for n in (0, 1):
        part = slice(n * STRETCH, (n + 1) * STRETCH)
        within = dot(lower.astype(F32).astype(BF16), log_gates[part])
        total = within[STRETCH - 1 : STRETCH]
        column = dot_exact(
            log_gates[part], jnp.ones((STRETCH, WIDTH), F32), 0, 0
        )
        stretches.append((part, within, total, jnp.exp(column)))
    states, pushes, tails = [start], [], []
    for part, within, total, decay in stretches:
        tail = jnp.exp(total - within)
        tails.append(tail)
        growth = dot_exact(k[part] * tail, values[part], 0, 0)
        states.append(decay * states[-1] + growth)
        pushes.append(dot_exact(q[part] * jnp.exp(within), grad_output[part], 0, 0))
    ends = [pushes[1], None]
    grad_q, grad_k, grad_v = [], [], []
    for n, (part, within, total, decay) in enumerate(stretches):
        up, down = jnp.exp(within), jnp.exp(-within)
        query_up, key_down = q[part] * up, k[part] * down
        go, v = grad_output[part], values[part]
        scores = jnp.where(lower, dot(go, v, 1, 1), 0.0)
        grad_q.append(up * (dot_exact(go, states[n], 1, 1) + dot_exact(scores, key_down)))
        grad = down * dot_exact(scores, query_up, 0, 0)
        weights = jnp.where(lower, dot_exact(query_up, key_down, 1, 1), 0.0)
        grad_value = dot_exact(weights, go, 0, 0)
        if ends[n] is not None:
            grad = grad + tails[n] * dot_exact(v, ends[n], 1, 1)
            grad_value = grad_value + dot_exact(k[part] * tails[n], ends[n])
        grad_k.append(grad)
        grad_v.append(grad_value)
    grad_q, grad_k = jnp.concatenate(grad_q, axis=0), jnp.concatenate(grad_k, axis=0)
    upper = ordered(LEN, lambda r, c: r <= c).astype(F32)
    gate = dot_exact(upper, q * grad_q - k * grad_k)
    tail = jnp.concatenate([tails[0] * jnp.exp(stretches[1][2]), tails[1]], axis=0)
    return grad_q.astype(BF16), grad_k, jnp.concatenate(grad_v, axis=0), gate, tail, states[2]


def final_of(end, values, key_rows, tail, grad_k, grad_v, gate, last):
    added = tail * dot(values, end, 1, 1)
    k = key_rows.astype(F32)
    grad_value = grad_v + dot_left(k * tail, end)
    upper = ordered(LEN, lambda r, c: r <= c).astype(F32).astype(BF16)
    own = dot_right(jnp.ones((8, WIDTH), BF16), end.astype(F32) * last, 1, 1)[:1]
    gate = gate - dot_right(upper, k * added) + own
    return (grad_k + added).astype(BF16), grad_value.astype(BF16), gate.astype(BF16)


def push_kernel(queries, log_gates, grad_output, out):
    out[...] = push_of(queries[...], log_gates[...], grad_output[...])


def group_kernel(place, got, out):
    runs = group_of(got, place[0])
    for y in range(4):
        for zh in range(FAR):
            out[zh, y] = runs[y]


def ends_kernel(place, near, far, out):
    ends = ends_of(near, far, place[0], place[1])
    for i in range(NEAR):
        out[i] = ends[i]


def local_kernel(queries, key_rows, values, log_gates, grad_output, start, grad_q, grad_k, grad_v, gate, tail, last):
    for h in range(HEADS):
        at = slice(h * WIDTH, (h + 1) * WIDTH)
        results = local_of(
            queries[:, at], key_rows[:, at], values[:, at], log_gates[:, at], grad_output[:, at], start[0, h]
        )
        for ref, value in zip((grad_q, grad_k, grad_v, gate, tail), results):
            ref[:, at] = value
        last[h] = results[5]


def final_kernel(
    ends, values, key_rows, tail, grad_k, grad_v, gate, last, inputs, before, out_k, out_gate, out_v, taps, padded
):
    padded[:8] = before[...].astype(F32)
    padded[8:] = inputs[...].astype(F32)
    every = ends[...].astype(F32)
    for h in range(HEADS):
        at = slice(h * WIDTH, (h + 1) * WIDTH)
        end = every[:, 8 * h : 8 * h + 8].reshape(LEN, WIDTH).astype(BF16)
        grad_key, grad_value, grad_gate = final_of(
            end, values[:, at], key_rows[:, at], tail[:, at], grad_k[:, at], grad_v[:, at], gate[:, at], last[h]
        )
        out_k[:, at] = grad_key
        out_v[:, at] = grad_value
        out_gate[:, at] = grad_gate
        rounded = grad_value.astype(F32)
        for tap in range(TAPS):
            term = jnp.sum(padded[8 - tap : 8 - tap + LEN, at] * rounded, axis=0, keepdims=True)
            taps[:, tap : tap + 1, at] = jnp.broadcast_to(term[None], (NEAR, 1, WIDTH))


def conv_kernel_body(place, grad_v, after, weights, *outs):
    outs, padded, rows = outs[:PEERS], outs[PEERS], outs[PEERS + 1]
    padded[:LEN] = grad_v[...].astype(F32)
    padded[LEN:] = after[...].astype(F32)
    total = weights[0:1] * padded[0:LEN]
    for tap in range(1, TAPS):
        total = total + weights[tap : tap + 1] * padded[tap : tap + LEN]
    rows[...] = total.reshape(PEERS, LEN // PEERS, HEADS * WIDTH)
    for r in range(PEERS):
        outs[r][...] = rows[place[2] ^ r].astype(BF16)


def join_kernel(place, *refs):
    out = refs[PEERS]
    for r in range(PEERS):
        start = pl.multiple_of((place[2] ^ r) * (HEADS * WIDTH), WIDTH)
        out[:, pl.ds(start, HEADS * WIDTH)] = refs[r][...]


def spread_kernel(got, out):
    total = jnp.sum(got[...], axis=0)
    out[...] = jnp.broadcast_to(total[None], out.shape)


def total_kernel(got, out):
    out[...] = jnp.sum(got[...], axis=0)


def call(kernel, outs, scalars=0, scratch=()):
    shapes = [jax.ShapeDtypeStruct(shape, dtype) for shape, dtype in outs]
    vmem = pl.BlockSpec()

    def run(*args):
        return pl.pallas_call(
            kernel,
            out_shape=shapes,
            in_specs=[pl.BlockSpec(memory_space=pltpu.SMEM)] * scalars + [vmem] * (len(args) - scalars),
            out_specs=[vmem] * len(outs),
            scratch_shapes=list(scratch),
        )(*args)

    return run


def exchange(x, axis):
    return lax.all_to_all(x, axis, 0, 0, tiled=True)


def passed_along(x, by):
    count = lax.axis_size(SEQ)
    pairs = [(i, i + by) for i in range(count) if 0 <= i + by < count]
    return lax.ppermute(x, SEQ, pairs)


def per_device(queries, key_rows, values, conv_input, log_gates, grad_output, saved_state, conv_kernel):
    columns = HEADS * WIDTH
    wide = (LEN, columns)
    place = jnp.stack([lax.axis_index(GROUP), lax.axis_index("zh"), lax.axis_index(HEAD)]).astype(jnp.int32)
    (sent,) = call(push_kernel, [((NEAR, ROWS, WIDTH), BF16)])(queries, log_gates, grad_output)
    near = exchange(sent, GROUP)
    (sent,) = call(group_kernel, [((FAR, 4, ROWS, WIDTH), BF16)], 1)(place, near)
    far = exchange(sent, "zh")
    locals_ = call(
        local_kernel, [(wide, BF16), (wide, F32), (wide, F32), (wide, F32), (wide, F32), ((HEADS, WIDTH, WIDTH), F32)]
    )(queries, key_rows, values, log_gates, grad_output, saved_state)
    before = passed_along(conv_input[-8:], 1)
    near, before, locals_ = lax.optimization_barrier((near, before, locals_))
    grad_queries, grad_k, grad_v, gate, tail, last = locals_
    (sent,) = call(ends_kernel, [((NEAR, 8 * HEADS, WIDTH), BF16)], 1)(place, near, far)
    ends = exchange(sent, GROUP)
    weights = lax.dynamic_slice_in_dim(conv_kernel, lax.axis_index(HEAD) * columns, columns, 1)
    grad_keys, grad_gates, grad_rows, taps = call(
        final_kernel,
        [(wide, BF16), (wide, BF16), (wide, BF16), ((NEAR, TAPS, columns), F32)],
        scratch=[pltpu.VMEM((LEN + 8, columns), F32)],
    )(ends, values, key_rows, tail, grad_k, grad_v, gate, last, conv_input, before)
    (taps,) = call(spread_kernel, [((FAR, TAPS, columns), F32)])(exchange(taps, GROUP))
    summed = exchange(taps, "zh")
    after = passed_along(grad_rows[:8], -1)
    piece = (LEN // PEERS, columns)
    pieces = call(
        conv_kernel_body,
        [(piece, BF16)] * PEERS,
        1,
        [pltpu.VMEM((LEN + 8, columns), F32), pltpu.VMEM((PEERS,) + piece, F32)],
    )(place, grad_rows, after, weights)
    pieces = list(pieces[:1]) + [
        lax.ppermute(pieces[r], HEAD, [(i, i ^ r) for i in range(PEERS)]) for r in range(1, PEERS)
    ]
    (grad_input,) = call(join_kernel, [((LEN // PEERS, PEERS * columns), BF16)], 1)(place, *pieces)
    (grad_kernel,) = call(total_kernel, [((TAPS, columns), F32)])(summed)
    return (grad_queries, grad_keys, grad_gates, grad_input, grad_kernel)


def solution(mesh):
    fine = Mesh(mesh.devices.reshape(4, FAR, 4, 4, 2), SEQ + HEAD)
    rows = P(SEQ, HEAD)
    return jax.shard_map(
        per_device,
        mesh=fine,
        in_specs=(rows, rows, rows, rows, rows, rows, P(SEQ, HEAD, None, None), P()),
        out_specs=(rows, rows, rows, P(SEQ + HEAD, None), P(None, HEAD)),
        check_vma=False,
    )
```

```python
import jax
import jax.numpy as jnp
from jax import lax
from jax.experimental import pallas as pl
from jax.experimental.pallas import tpu as pltpu
from jax.sharding import Mesh, PartitionSpec as P

HEADS = 3
WIDTH = 128
LEN = 128
STRETCH = 64
TAPS = 4
NEAR = 16
FAR = 8
PEERS = 8
ROWS = 32
OWN = 8 * HEADS
FAR_ROWS = 4 * OWN + 8
APART = 40
SEQ = ("y", "zh", "zl")
HEAD = ("x", "core")
GROUP = ("y", "zl")
F32 = jnp.float32
BF16 = jnp.bfloat16
PRECISE = lax.Precision.HIGHEST


def dot(a, b, over_a=1, over_b=0, precision=None):
    return lax.dot_general(
        a, b, (((over_a,), (over_b,)), ((), ())), precision=precision, preferred_element_type=F32
    )


def dot_exact(a, b, over_a=1, over_b=0):
    return dot(a.astype(F32), b.astype(F32), over_a, over_b, PRECISE)


def two_parts(a):
    high = a.astype(BF16)
    return high, (a - high.astype(F32)).astype(BF16)


def dot_left(a, b, over_a=1, over_b=0):
    high, low = two_parts(a)
    return dot(high, b, over_a, over_b) + dot(low, b, over_a, over_b)


def dot_right(a, b, over_a=1, over_b=0):
    high, low = two_parts(b)
    return dot(a, high, over_a, over_b) + dot(a, low, over_a, over_b)


def ordered(size, compare):
    row = lax.broadcasted_iota(jnp.int32, (size, size), 0)
    column = lax.broadcasted_iota(jnp.int32, (size, size), 1)
    return compare(row, column)


def head_of(x, h):
    return x[:, h * WIDTH : (h + 1) * WIDTH]


def tail_rows(logs):
    row = lax.broadcasted_iota(jnp.int32, (8, WIDTH), 0)
    tail = jnp.zeros((8, WIDTH), F32)
    for h in range(HEADS):
        high = logs[h].astype(BF16).astype(F32)
        low = logs[h] - high
        tail = jnp.where(row == h, high, tail)
        tail = jnp.where(row == HEADS + h, low, tail)
    return tail


def push_of(queries, log_gates, grad_output):
    lower = ordered(LEN, lambda r, c: r >= c).astype(F32).astype(BF16)
    within = dot(lower, log_gates)
    query_up = queries.astype(F32) * jnp.exp(within)
    pushes = [
        dot_left(head_of(query_up, h), head_of(grad_output, h), 0, 0).reshape(NEAR, 8, WIDTH)
        for h in range(HEADS)
    ]
    last = within[LEN - 1 : LEN]
    tail = tail_rows([head_of(last, h) for h in range(HEADS)])
    tail = jnp.broadcast_to(tail[None], (NEAR, 8, WIDTH))
    return jnp.concatenate(pushes + [tail], axis=1).astype(BF16)


def logs_of(tail):
    return [tail[h : h + 1] + tail[HEADS + h : HEADS + h + 1] for h in range(HEADS)]


def decays_of(logs, place, step=0):
    lane = lax.broadcasted_iota(jnp.int32, (8, WIDTH), 1)
    row = lax.broadcasted_iota(jnp.int32, (8, WIDTH), 0) + 8 * place
    decays = []
    for h in range(HEADS):
        mine = lane == ((row + step * h) & (WIDTH - 1))
        picked = jnp.sum(jnp.where(mine, logs[h], 0.0), axis=1, keepdims=True)
        decays.append(jnp.broadcast_to(jnp.exp(picked), (8, WIDTH)))
    return jnp.concatenate(decays, axis=0)


def run_of(got, place):
    x = got.astype(F32)
    logs = logs_of(x[OWN:])
    return x[:OWN], decays_of(logs, place), logs


def packed_of(totals, place):
    lane = lax.broadcasted_iota(jnp.int32, (8, WIDTH), 1)
    row = lax.broadcasted_iota(jnp.int32, (8, WIDTH), 0)
    packed = jnp.zeros((8, WIDTH), F32)
    for h in range(HEADS):
        rows = jnp.zeros((8, WIDTH), F32)
        for y in range(4):
            high = totals[y][h].astype(BF16).astype(F32)
            rows = jnp.where(row == 2 * y, high, rows)
            rows = jnp.where(row == 2 * y + 1, totals[y][h] - high, rows)
        rows = jnp.where((lane >> 3) == place, rows, 0.0)
        packed = packed + (pltpu.roll(rows, APART * h, 1) if h else rows)
    return packed


def group_of(got, place):
    runs, totals = [], []
    for y in range(4):
        running = jnp.zeros((OWN, WIDTH), F32)
        total = [jnp.zeros((1, WIDTH), F32)] * HEADS
        for zl in (3, 2, 1, 0):
            push, decay, logs = run_of(got[y * 4 + zl], place)
            running = push + decay * running
            total = [a + b for a, b in zip(total, logs)]
        runs.append(running)
        totals.append(total)
    return jnp.concatenate(runs + [packed_of(totals, place)], axis=0).astype(BF16)


def ends_of(near, far, place, mine):
    ends = [None] * NEAR
    every = [far[zh].astype(F32) for zh in range(FAR)]
    running = jnp.zeros((OWN, WIDTH), F32)
    for y in (3, 2, 1, 0):
        entering = jnp.zeros((OWN, WIDTH), F32)
        for zh in range(FAR - 1, -1, -1):
            entering = jnp.where(mine == zh, running, entering)
            at = 4 * OWN + 2 * y
            logs = every[zh][at : at + 1] + every[zh][at + 1 : at + 2]
            decay = decays_of([logs] * HEADS, place, APART)
            running = every[zh][y * OWN : (y + 1) * OWN] + decay * running
        for zl in (3, 2, 1, 0):
            ends[y * 4 + zl] = entering.astype(BF16)
            push, decay, _ = run_of(near[y * 4 + zl], place)
            entering = push + decay * entering
    return ends


def local_of(queries, key_rows, values, log_gates, grad_output, start):
    q, k = queries.astype(F32), key_rows.astype(F32)
    lower = ordered(STRETCH, lambda r, c: r >= c)
    stretches = []
    for n in (0, 1):
        part = slice(n * STRETCH, (n + 1) * STRETCH)
        within = dot(lower.astype(F32).astype(BF16), log_gates[part])
        total = within[STRETCH - 1 : STRETCH]
        column = dot_exact(
            log_gates[part], jnp.ones((STRETCH, WIDTH), F32), 0, 0
        )
        stretches.append((part, within, total, jnp.exp(column)))
    states, pushes, tails = [start], [], []
    for part, within, total, decay in stretches:
        tail = jnp.exp(total - within)
        tails.append(tail)
        growth = dot_exact(k[part] * tail, values[part], 0, 0)
        states.append(decay * states[-1] + growth)
        pushes.append(dot_exact(q[part] * jnp.exp(within), grad_output[part], 0, 0))
    ends = [pushes[1], None]
    grad_q, grad_k, grad_v = [], [], []
    for n, (part, within, total, decay) in enumerate(stretches):
        up, down = jnp.exp(within), jnp.exp(-within)
        query_up, key_down = q[part] * up, k[part] * down
        go, v = grad_output[part], values[part]
        scores = jnp.where(lower, dot(go, v, 1, 1), 0.0)
        grad_q.append(up * (dot_exact(go, states[n], 1, 1) + dot_exact(scores, key_down)))
        grad = down * dot_exact(scores, query_up, 0, 0)
        weights = jnp.where(lower, dot_exact(query_up, key_down, 1, 1), 0.0)
        grad_value = dot_exact(weights, go, 0, 0)
        if ends[n] is not None:
            grad = grad + tails[n] * dot_exact(v, ends[n], 1, 1)
            grad_value = grad_value + dot_exact(k[part] * tails[n], ends[n])
        grad_k.append(grad)
        grad_v.append(grad_value)
    grad_q, grad_k = jnp.concatenate(grad_q, axis=0), jnp.concatenate(grad_k, axis=0)
    upper = ordered(LEN, lambda r, c: r <= c).astype(F32)
    gate = dot_exact(upper, q * grad_q - k * grad_k)
    tail = jnp.concatenate([tails[0] * jnp.exp(stretches[1][2]), tails[1]], axis=0)
    return grad_q.astype(BF16), grad_k, jnp.concatenate(grad_v, axis=0), gate, tail, states[2]


def final_of(end, values, key_rows, tail, grad_k, grad_v, gate, last):
    added = tail * dot(values, end, 1, 1)
    k = key_rows.astype(F32)
    grad_value = grad_v + dot_left(k * tail, end)
    upper = ordered(LEN, lambda r, c: r <= c).astype(F32).astype(BF16)
    own = dot_right(jnp.ones((8, WIDTH), BF16), end.astype(F32) * last, 1, 1)[:1]
    gate = gate - dot_right(upper, k * added) + own
    return (grad_k + added).astype(BF16), grad_value.astype(BF16), gate.astype(BF16)


def push_kernel(queries, log_gates, grad_output, out):
    out[...] = push_of(queries[...], log_gates[...], grad_output[...])


def group_kernel(place, got, out):
    runs = group_of(got, place[0])
    for zh in range(FAR):
        out[zh] = runs


def ends_kernel(place, near, far, out):
    ends = ends_of(near, far, place[0], place[1])
    for i in range(NEAR):
        out[i] = ends[i]


def local_kernel(queries, key_rows, values, log_gates, grad_output, start, grad_q, grad_k, grad_v, gate, tail, last):
    for h in range(HEADS):
        at = slice(h * WIDTH, (h + 1) * WIDTH)
        results = local_of(
            queries[:, at], key_rows[:, at], values[:, at], log_gates[:, at], grad_output[:, at], start[0, h]
        )
        for ref, value in zip((grad_q, grad_k, grad_v, gate, tail), results):
            ref[:, at] = value
        last[h] = results[5]


def final_kernel(
    ends, values, key_rows, tail, grad_k, grad_v, gate, last, inputs, before, out_k, out_gate, out_v, taps, padded
):
    padded[:8] = before[...].astype(F32)
    padded[8:] = inputs[...].astype(F32)
    every = ends[...].astype(F32)
    for h in range(HEADS):
        at = slice(h * WIDTH, (h + 1) * WIDTH)
        end = every[:, 8 * h : 8 * h + 8].reshape(LEN, WIDTH).astype(BF16)
        grad_key, grad_value, grad_gate = final_of(
            end, values[:, at], key_rows[:, at], tail[:, at], grad_k[:, at], grad_v[:, at], gate[:, at], last[h]
        )
        out_k[:, at] = grad_key
        out_v[:, at] = grad_value
        out_gate[:, at] = grad_gate
        rounded = grad_value.astype(F32)
        for tap in range(TAPS):
            term = jnp.sum(padded[8 - tap : 8 - tap + LEN, at] * rounded, axis=0, keepdims=True)
            taps[:, tap : tap + 1, at] = jnp.broadcast_to(term[None], (NEAR, 1, WIDTH))


def conv_kernel_body(place, grad_v, after, weights, *outs):
    outs, padded, rows = outs[:PEERS], outs[PEERS], outs[PEERS + 1]
    padded[:LEN] = grad_v[...].astype(F32)
    padded[LEN:] = after[...].astype(F32)
    total = weights[0:1] * padded[0:LEN]
    for tap in range(1, TAPS):
        total = total + weights[tap : tap + 1] * padded[tap : tap + LEN]
    rows[...] = total.reshape(PEERS, LEN // PEERS, HEADS * WIDTH)
    for r in range(PEERS):
        outs[r][...] = rows[place[2] ^ r].astype(BF16)


def join_kernel(place, *refs):
    out = refs[PEERS]
    for r in range(PEERS):
        start = pl.multiple_of((place[2] ^ r) * (HEADS * WIDTH), WIDTH)
        out[:, pl.ds(start, HEADS * WIDTH)] = refs[r][...]


def spread_kernel(got, out):
    total = jnp.sum(got[...], axis=0)
    out[...] = jnp.broadcast_to(total[None], out.shape)


def total_kernel(got, out):
    out[...] = jnp.sum(got[...], axis=0)


def call(kernel, outs, scalars=0, scratch=()):
    shapes = [jax.ShapeDtypeStruct(shape, dtype) for shape, dtype in outs]
    vmem = pl.BlockSpec()

    def run(*args):
        return pl.pallas_call(
            kernel,
            out_shape=shapes,
            in_specs=[pl.BlockSpec(memory_space=pltpu.SMEM)] * scalars + [vmem] * (len(args) - scalars),
            out_specs=[vmem] * len(outs),
            scratch_shapes=list(scratch),
        )(*args)

    return run


def exchange(x, axis):
    return lax.all_to_all(x, axis, 0, 0, tiled=True)


def passed_along(x, by):
    count = lax.axis_size(SEQ)
    pairs = [(i, i + by) for i in range(count) if 0 <= i + by < count]
    return lax.ppermute(x, SEQ, pairs)


def per_device(queries, key_rows, values, conv_input, log_gates, grad_output, saved_state, conv_kernel):
    columns = HEADS * WIDTH
    wide = (LEN, columns)
    place = jnp.stack([lax.axis_index(GROUP), lax.axis_index("zh"), lax.axis_index(HEAD)]).astype(jnp.int32)
    (sent,) = call(push_kernel, [((NEAR, ROWS, WIDTH), BF16)])(queries, log_gates, grad_output)
    near = exchange(sent, GROUP)
    (sent,) = call(group_kernel, [((FAR, FAR_ROWS, WIDTH), BF16)], 1)(place, near)
    far = exchange(sent, "zh")
    locals_ = call(
        local_kernel, [(wide, BF16), (wide, F32), (wide, F32), (wide, F32), (wide, F32), ((HEADS, WIDTH, WIDTH), F32)]
    )(queries, key_rows, values, log_gates, grad_output, saved_state)
    before = passed_along(conv_input[-8:], 1)
    near, before, locals_ = lax.optimization_barrier((near, before, locals_))
    grad_queries, grad_k, grad_v, gate, tail, last = locals_
    (sent,) = call(ends_kernel, [((NEAR, OWN, WIDTH), BF16)], 1)(place, near, far)
    ends = exchange(sent, GROUP)
    weights = lax.dynamic_slice_in_dim(conv_kernel, lax.axis_index(HEAD) * columns, columns, 1)
    grad_keys, grad_gates, grad_rows, taps = call(
        final_kernel,
        [(wide, BF16), (wide, BF16), (wide, BF16), ((NEAR, TAPS, columns), F32)],
        scratch=[pltpu.VMEM((LEN + 8, columns), F32)],
    )(ends, values, key_rows, tail, grad_k, grad_v, gate, last, conv_input, before)
    (taps,) = call(spread_kernel, [((FAR, TAPS, columns), F32)])(exchange(taps, GROUP))
    summed = exchange(taps, "zh")
    after = passed_along(grad_rows[:8], -1)
    piece = (LEN // PEERS, columns)
    pieces = call(
        conv_kernel_body,
        [(piece, BF16)] * PEERS,
        1,
        [pltpu.VMEM((LEN + 8, columns), F32), pltpu.VMEM((PEERS,) + piece, F32)],
    )(place, grad_rows, after, weights)
    sent, pieces = pieces, [pieces[0]]
    for r in range(1, PEERS):
        pieces.append(lax.ppermute(sent[r], HEAD, [(i, i ^ r) for i in range(PEERS)]))
    (grad_input,) = call(join_kernel, [((LEN // PEERS, PEERS * columns), BF16)], 1)(place, *pieces)
    (grad_kernel,) = call(total_kernel, [((TAPS, columns), F32)])(summed)
    return (grad_queries, grad_keys, grad_gates, grad_input, grad_kernel)


def solution(mesh):
    fine = Mesh(mesh.devices.reshape(4, FAR, 4, 4, 2), SEQ + HEAD)
    rows = P(SEQ, HEAD)
    return jax.shard_map(
        per_device,
        mesh=fine,
        in_specs=(rows, rows, rows, rows, rows, rows, P(SEQ, HEAD, None, None), P()),
        out_specs=(rows, rows, rows, P(SEQ + HEAD, None), P(None, HEAD)),
        check_vma=False,
    )
```

```python
import jax
import jax.numpy as jnp
from jax import lax
from jax.experimental import pallas as pl
from jax.experimental.pallas import tpu as pltpu
from jax.sharding import Mesh, PartitionSpec as P

HEADS = 3
WIDTH = 128
LEN = 128
STRETCH = 64
TAPS = 4
NEAR = 16
FAR = 8
PEERS = 8
ROWS = 32
OWN = 8 * HEADS
FAR_ROWS = 4 * OWN + 8
APART = 40
SEQ = ("y", "zh", "zl")
HEAD = ("x", "core")
GROUP = ("y", "zl")
F32 = jnp.float32
BF16 = jnp.bfloat16
PRECISE = lax.Precision.HIGHEST


def dot(a, b, over_a=1, over_b=0, precision=None):
    return lax.dot_general(
        a, b, (((over_a,), (over_b,)), ((), ())), precision=precision, preferred_element_type=F32
    )


def dot_exact(a, b, over_a=1, over_b=0):
    return dot(a.astype(F32), b.astype(F32), over_a, over_b, PRECISE)


def two_parts(a):
    high = a.astype(BF16)
    return high, (a - high.astype(F32)).astype(BF16)


def dot_left(a, b, over_a=1, over_b=0):
    high, low = two_parts(a)
    return dot(high, b, over_a, over_b) + dot(low, b, over_a, over_b)


def dot_right(a, b, over_a=1, over_b=0):
    high, low = two_parts(b)
    return dot(a, high, over_a, over_b) + dot(a, low, over_a, over_b)


def ordered(size, compare):
    row = lax.broadcasted_iota(jnp.int32, (size, size), 0)
    column = lax.broadcasted_iota(jnp.int32, (size, size), 1)
    return compare(row, column)


def head_of(x, h):
    return x[:, h * WIDTH : (h + 1) * WIDTH]


def tail_rows(logs):
    row = lax.broadcasted_iota(jnp.int32, (8, WIDTH), 0)
    tail = jnp.zeros((8, WIDTH), F32)
    for h in range(HEADS):
        high = logs[h].astype(BF16).astype(F32)
        low = logs[h] - high
        tail = jnp.where(row == h, high, tail)
        tail = jnp.where(row == HEADS + h, low, tail)
    return tail


def push_of(queries, log_gates, grad_output):
    lower = ordered(LEN, lambda r, c: r >= c).astype(F32).astype(BF16)
    within = dot(lower, log_gates)
    query_up = queries.astype(F32) * jnp.exp(within)
    pushes = [
        dot_left(head_of(query_up, h), head_of(grad_output, h), 0, 0).reshape(NEAR, 8, WIDTH)
        for h in range(HEADS)
    ]
    last = within[LEN - 1 : LEN]
    tail = tail_rows([head_of(last, h) for h in range(HEADS)])
    tail = jnp.broadcast_to(tail[None], (NEAR, 8, WIDTH))
    return jnp.concatenate(pushes + [tail], axis=1).astype(BF16)


def logs_of(tail):
    return [tail[h : h + 1] + tail[HEADS + h : HEADS + h + 1] for h in range(HEADS)]


def decays_of(logs, place, step=0):
    lane = lax.broadcasted_iota(jnp.int32, (8, WIDTH), 1)
    row = lax.broadcasted_iota(jnp.int32, (8, WIDTH), 0) + 8 * place
    decays = []
    for h in range(HEADS):
        mine = lane == ((row + step * h) & (WIDTH - 1))
        picked = jnp.sum(jnp.where(mine, logs[h], 0.0), axis=1, keepdims=True)
        decays.append(jnp.broadcast_to(jnp.exp(picked), (8, WIDTH)))
    return jnp.concatenate(decays, axis=0)


def run_of(got, place):
    x = got.astype(F32)
    logs = logs_of(x[OWN:])
    return x[:OWN], decays_of(logs, place), logs


def packed_of(totals, place):
    lane = lax.broadcasted_iota(jnp.int32, (8, WIDTH), 1)
    row = lax.broadcasted_iota(jnp.int32, (8, WIDTH), 0)
    packed = jnp.zeros((8, WIDTH), F32)
    for h in range(HEADS):
        rows = jnp.zeros((8, WIDTH), F32)
        for y in range(4):
            high = totals[y][h].astype(BF16).astype(F32)
            rows = jnp.where(row == 2 * y, high, rows)
            rows = jnp.where(row == 2 * y + 1, totals[y][h] - high, rows)
        rows = jnp.where((lane >> 3) == place, rows, 0.0)
        packed = packed + (pltpu.roll(rows, APART * h, 1) if h else rows)
    return packed


def group_of(got, place):
    runs, totals = [], []
    for y in range(4):
        running = jnp.zeros((OWN, WIDTH), F32)
        total = [jnp.zeros((1, WIDTH), F32)] * HEADS
        for zl in (3, 2, 1, 0):
            push, decay, logs = run_of(got[y * 4 + zl], place)
            running = push + decay * running
            total = [a + b for a, b in zip(total, logs)]
        runs.append(running)
        totals.append(total)
    return jnp.concatenate(runs + [packed_of(totals, place)], axis=0).astype(BF16)


def ends_of(near, far, place, mine):
    ends = [None] * NEAR
    every = [far[zh].astype(F32) for zh in range(FAR)]
    running = jnp.zeros((OWN, WIDTH), F32)
    for y in (3, 2, 1, 0):
        entering = jnp.zeros((OWN, WIDTH), F32)
        for zh in range(FAR - 1, -1, -1):
            entering = jnp.where(mine == zh, running, entering)
            at = 4 * OWN + 2 * y
            logs = every[zh][at : at + 1] + every[zh][at + 1 : at + 2]
            decay = decays_of([logs] * HEADS, place, APART)
            running = every[zh][y * OWN : (y + 1) * OWN] + decay * running
        for zl in (3, 2, 1, 0):
            ends[y * 4 + zl] = entering.astype(BF16)
            push, decay, _ = run_of(near[y * 4 + zl], place)
            entering = push + decay * entering
    return ends


def local_of(queries, key_rows, values, log_gates, grad_output, start):
    q, k = queries.astype(F32), key_rows.astype(F32)
    lower = ordered(STRETCH, lambda r, c: r >= c)
    stretches = []
    for n in (0, 1):
        part = slice(n * STRETCH, (n + 1) * STRETCH)
        within = dot(lower.astype(F32).astype(BF16), log_gates[part])
        total = within[STRETCH - 1 : STRETCH]
        column = dot_exact(
            log_gates[part], jnp.ones((STRETCH, WIDTH), F32), 0, 0
        )
        stretches.append((part, within, total, jnp.exp(column)))
    states, pushes, tails = [start], [], []
    for part, within, total, decay in stretches:
        tail = jnp.exp(total - within)
        tails.append(tail)
        growth = dot_exact(k[part] * tail, values[part], 0, 0)
        states.append(decay * states[-1] + growth)
        pushes.append(dot_exact(q[part] * jnp.exp(within), grad_output[part], 0, 0))
    ends = [pushes[1], None]
    grad_q, grad_k, grad_v = [], [], []
    for n, (part, within, total, decay) in enumerate(stretches):
        up, down = jnp.exp(within), jnp.exp(-within)
        query_up, key_down = q[part] * up, k[part] * down
        go, v = grad_output[part], values[part]
        scores = jnp.where(lower, dot(go, v, 1, 1), 0.0)
        grad_q.append(up * (dot_exact(go, states[n], 1, 1) + dot_exact(scores, key_down)))
        grad = down * dot_exact(scores, query_up, 0, 0)
        weights = jnp.where(lower, dot_exact(query_up, key_down, 1, 1), 0.0)
        grad_value = dot_exact(weights, go, 0, 0)
        if ends[n] is not None:
            grad = grad + tails[n] * dot_exact(v, ends[n], 1, 1)
            grad_value = grad_value + dot_exact(k[part] * tails[n], ends[n])
        grad_k.append(grad)
        grad_v.append(grad_value)
    grad_q, grad_k = jnp.concatenate(grad_q, axis=0), jnp.concatenate(grad_k, axis=0)
    upper = ordered(LEN, lambda r, c: r <= c).astype(F32)
    gate = dot_exact(upper, q * grad_q - k * grad_k)
    tail = jnp.concatenate([tails[0] * jnp.exp(stretches[1][2]), tails[1]], axis=0)
    return grad_q.astype(BF16), grad_k, jnp.concatenate(grad_v, axis=0), gate, tail, states[2]


def final_of(end, values, key_rows, tail, grad_k, grad_v, gate, last):
    added = tail * dot(values, end, 1, 1)
    k = key_rows.astype(F32)
    grad_value = grad_v + dot_left(k * tail, end)
    upper = ordered(LEN, lambda r, c: r <= c).astype(F32).astype(BF16)
    own = dot_right(jnp.ones((8, WIDTH), BF16), end.astype(F32) * last, 1, 1)[:1]
    gate = gate - dot_right(upper, k * added) + own
    return (grad_k + added).astype(BF16), grad_value.astype(BF16), gate.astype(BF16)


def push_kernel(queries, log_gates, grad_output, out):
    out[...] = push_of(queries[...], log_gates[...], grad_output[...])


def group_kernel(place, got, out):
    runs = group_of(got, place[0])
    for zh in range(FAR):
        out[zh] = runs


def ends_kernel(place, near, far, out):
    ends = ends_of(near, far, place[0], place[1])
    for i in range(NEAR):
        out[i] = ends[i]


def local_kernel(queries, key_rows, values, log_gates, grad_output, start, grad_q, grad_k, grad_v, gate, tail, last):
    for h in range(HEADS):
        at = slice(h * WIDTH, (h + 1) * WIDTH)
        results = local_of(
            queries[:, at], key_rows[:, at], values[:, at], log_gates[:, at], grad_output[:, at], start[0, h]
        )
        for ref, value in zip((grad_q, grad_k, grad_v, gate, tail), results):
            ref[:, at] = value
        last[h] = results[5]


def final_kernel(
    ends, values, key_rows, tail, grad_k, grad_v, gate, last, inputs, before, out_k, out_gate, out_v, taps, padded
):
    padded[:8] = before[...].astype(F32)
    padded[8:] = inputs[...].astype(F32)
    every = ends[...].astype(F32)
    for h in range(HEADS):
        at = slice(h * WIDTH, (h + 1) * WIDTH)
        end = every[:, 8 * h : 8 * h + 8].reshape(LEN, WIDTH).astype(BF16)
        grad_key, grad_value, grad_gate = final_of(
            end, values[:, at], key_rows[:, at], tail[:, at], grad_k[:, at], grad_v[:, at], gate[:, at], last[h]
        )
        out_k[:, at] = grad_key
        out_v[:, at] = grad_value
        out_gate[:, at] = grad_gate
        rounded = grad_value.astype(F32)
        for tap in range(TAPS):
            term = jnp.sum(padded[8 - tap : 8 - tap + LEN, at] * rounded, axis=0, keepdims=True)
            taps[:, tap : tap + 1, at] = jnp.broadcast_to(term[None], (NEAR, 1, WIDTH))


def conv_kernel_body(place, grad_v, after, weights, mine, other, padded, rows):
    padded[:LEN] = grad_v[...].astype(F32)
    padded[LEN:] = after[...].astype(F32)
    total = weights[0:1] * padded[0:LEN]
    for tap in range(1, TAPS):
        total = total + weights[tap : tap + 1] * padded[tap : tap + LEN]
    rows[...] = total.reshape(PEERS, LEN // PEERS, HEADS * WIDTH)
    for r in range(PEERS // 2):
        mine[r] = rows[place[2] ^ (2 * r)].astype(BF16)
        other[r] = rows[place[2] ^ (2 * r + 1)].astype(BF16)


def pack_kernel(mine, other, *outs):
    for r in range(1, PEERS // 2):
        outs[r - 1][0] = mine[r]
        outs[r - 1][1] = other[r]


def join_kernel(place, mine, other, *refs):
    out = refs[PEERS // 2 - 1]
    for r in range(PEERS // 2):
        for core in (0, 1):
            if r:
                piece = refs[r - 1][core]
            else:
                piece = (mine, other)[core][0]
            start = pl.multiple_of((place[2] ^ (2 * r + core)) * (HEADS * WIDTH), WIDTH)
            out[:, pl.ds(start, HEADS * WIDTH)] = piece


def call(kernel, outs, scalars=0, scratch=()):
    shapes = [jax.ShapeDtypeStruct(shape, dtype) for shape, dtype in outs]
    vmem = pl.BlockSpec()

    def run(*args):
        return pl.pallas_call(
            kernel,
            out_shape=shapes,
            in_specs=[pl.BlockSpec(memory_space=pltpu.SMEM)] * scalars + [vmem] * (len(args) - scalars),
            out_specs=[vmem] * len(outs),
            scratch_shapes=list(scratch),
        )(*args)

    return run


def exchange(x, axis):
    return lax.all_to_all(x, axis, 0, 0, tiled=True)


def passed_along(x, by):
    count = lax.axis_size(SEQ)
    pairs = [(i, i + by) for i in range(count) if 0 <= i + by < count]
    return lax.ppermute(x, SEQ, pairs)


def per_device(queries, key_rows, values, conv_input, log_gates, grad_output, saved_state, conv_kernel):
    columns = HEADS * WIDTH
    wide = (LEN, columns)
    place = jnp.stack([lax.axis_index(GROUP), lax.axis_index("zh"), lax.axis_index(HEAD)]).astype(jnp.int32)
    (sent,) = call(push_kernel, [((NEAR, ROWS, WIDTH), BF16)])(queries, log_gates, grad_output)
    near = exchange(sent, GROUP)
    (sent,) = call(group_kernel, [((FAR, FAR_ROWS, WIDTH), BF16)], 1)(place, near)
    far = exchange(sent, "zh")
    locals_ = call(
        local_kernel, [(wide, BF16), (wide, F32), (wide, F32), (wide, F32), (wide, F32), ((HEADS, WIDTH, WIDTH), F32)]
    )(queries, key_rows, values, log_gates, grad_output, saved_state)
    before = passed_along(conv_input[-8:], 1)
    near, before, locals_ = lax.optimization_barrier((near, before, locals_))
    grad_queries, grad_k, grad_v, gate, tail, last = locals_
    (sent,) = call(ends_kernel, [((NEAR, OWN, WIDTH), BF16)], 1)(place, near, far)
    ends = exchange(sent, GROUP)
    weights = lax.dynamic_slice_in_dim(conv_kernel, lax.axis_index(HEAD) * columns, columns, 1)
    grad_keys, grad_gates, grad_rows, taps = call(
        final_kernel,
        [(wide, BF16), (wide, BF16), (wide, BF16), ((NEAR, TAPS, columns), F32)],
        scratch=[pltpu.VMEM((LEN + 8, columns), F32)],
    )(ends, values, key_rows, tail, grad_k, grad_v, gate, last, conv_input, before)
    taps = jnp.sum(exchange(taps, GROUP), axis=0)
    summed = exchange(jnp.broadcast_to(taps[None], (FAR, TAPS, columns)), "zh")
    after = passed_along(grad_rows[:8], -1)
    piece = (LEN // PEERS, columns)
    half = PEERS // 2
    mine, other = call(
        conv_kernel_body,
        [((half,) + piece, BF16)] * 2,
        1,
        [pltpu.VMEM((LEN + 8, columns), F32), pltpu.VMEM((PEERS,) + piece, F32)],
    )(place, grad_rows, after, weights)
    other = lax.ppermute(other, HEAD, [(i, i ^ 1) for i in range(PEERS)])
    sent = call(pack_kernel, [((2,) + piece, BF16)] * (half - 1))(mine, other)
    pieces = [
        lax.ppermute(sent[r - 1], HEAD, [(i, i ^ (2 * r)) for i in range(PEERS)]) for r in range(1, half)
    ]
    (grad_input,) = call(join_kernel, [((LEN // PEERS, PEERS * columns), BF16)], 1)(place, mine, other, *pieces)
    grad_kernel = jnp.sum(summed, axis=0)
    return (grad_queries, grad_keys, grad_gates, grad_input, grad_kernel)


def solution(mesh):
    fine = Mesh(mesh.devices.reshape(4, FAR, 4, 4, 2), SEQ + HEAD)
    rows = P(SEQ, HEAD)
    return jax.shard_map(
        per_device,
        mesh=fine,
        in_specs=(rows, rows, rows, rows, rows, rows, P(SEQ, HEAD, None, None), P()),
        out_specs=(rows, rows, rows, P(SEQ + HEAD, None), P(None, HEAD)),
        check_vma=False,
    )
```

```python
import jax
import jax.numpy as jnp
from jax import lax
from jax.experimental import pallas as pl
from jax.experimental.pallas import tpu as pltpu
from jax.sharding import Mesh, PartitionSpec as P

HEADS = 3
WIDTH = 128
LEN = 128
STRETCH = 64
TAPS = 4
NEAR = 16
FAR = 8
PEERS = 8
ROWS = 32
OWN = 8 * HEADS
FAR_ROWS = 4 * OWN + 8
APART = 40
SEQ = ("y", "zh", "zl")
HEAD = ("x", "core")
GROUP = ("y", "zl")
F32 = jnp.float32
BF16 = jnp.bfloat16
PRECISE = lax.Precision.HIGHEST


def dot(a, b, over_a=1, over_b=0, precision=None):
    return lax.dot_general(
        a, b, (((over_a,), (over_b,)), ((), ())), precision=precision, preferred_element_type=F32
    )


def dot_exact(a, b, over_a=1, over_b=0):
    return dot(a.astype(F32), b.astype(F32), over_a, over_b, PRECISE)


def two_parts(a):
    high = a.astype(BF16)
    return high, (a - high.astype(F32)).astype(BF16)


def dot_left(a, b, over_a=1, over_b=0):
    high, low = two_parts(a)
    return dot(high, b, over_a, over_b) + dot(low, b, over_a, over_b)


def dot_right(a, b, over_a=1, over_b=0):
    high, low = two_parts(b)
    return dot(a, high, over_a, over_b) + dot(a, low, over_a, over_b)


def ordered(size, compare):
    row = lax.broadcasted_iota(jnp.int32, (size, size), 0)
    column = lax.broadcasted_iota(jnp.int32, (size, size), 1)
    return compare(row, column)


def head_of(x, h):
    return x[:, h * WIDTH : (h + 1) * WIDTH]


def tail_rows(logs):
    row = lax.broadcasted_iota(jnp.int32, (8, WIDTH), 0)
    tail = jnp.zeros((8, WIDTH), F32)
    for h in range(HEADS):
        high = logs[h].astype(BF16).astype(F32)
        low = logs[h] - high
        tail = jnp.where(row == h, high, tail)
        tail = jnp.where(row == HEADS + h, low, tail)
    return tail


def push_of(queries, log_gates, grad_output):
    lower = ordered(LEN, lambda r, c: r >= c).astype(F32).astype(BF16)
    within = dot(lower, log_gates)
    query_up = queries.astype(F32) * jnp.exp(within)
    pushes = [
        dot_left(head_of(query_up, h), head_of(grad_output, h), 0, 0).reshape(NEAR, 8, WIDTH)
        for h in range(HEADS)
    ]
    last = within[LEN - 1 : LEN]
    tail = tail_rows([head_of(last, h) for h in range(HEADS)])
    tail = jnp.broadcast_to(tail[None], (NEAR, 8, WIDTH))
    return jnp.concatenate(pushes + [tail], axis=1).astype(BF16)


def logs_of(tail):
    return [tail[h : h + 1] + tail[HEADS + h : HEADS + h + 1] for h in range(HEADS)]


def decays_of(logs, place, step=0):
    lane = lax.broadcasted_iota(jnp.int32, (8, WIDTH), 1)
    row = lax.broadcasted_iota(jnp.int32, (8, WIDTH), 0) + 8 * place
    decays = []
    for h in range(HEADS):
        mine = lane == ((row + step * h) & (WIDTH - 1))
        picked = jnp.sum(jnp.where(mine, logs[h], 0.0), axis=1, keepdims=True)
        decays.append(jnp.broadcast_to(jnp.exp(picked), (8, WIDTH)))
    return jnp.concatenate(decays, axis=0)


def run_of(got, place):
    x = got.astype(F32)
    logs = logs_of(x[OWN:])
    return x[:OWN], decays_of(logs, place), logs


def packed_of(totals, place):
    lane = lax.broadcasted_iota(jnp.int32, (8, WIDTH), 1)
    row = lax.broadcasted_iota(jnp.int32, (8, WIDTH), 0)
    packed = jnp.zeros((8, WIDTH), F32)
    for h in range(HEADS):
        rows = jnp.zeros((8, WIDTH), F32)
        for y in range(4):
            high = totals[y][h].astype(BF16).astype(F32)
            rows = jnp.where(row == 2 * y, high, rows)
            rows = jnp.where(row == 2 * y + 1, totals[y][h] - high, rows)
        rows = jnp.where((lane >> 3) == place, rows, 0.0)
        packed = packed + (pltpu.roll(rows, APART * h, 1) if h else rows)
    return packed


def group_of(got, place):
    runs, totals = [], []
    for y in range(4):
        running = jnp.zeros((OWN, WIDTH), F32)
        total = [jnp.zeros((1, WIDTH), F32)] * HEADS
        for zl in (3, 2, 1, 0):
            push, decay, logs = run_of(got[y * 4 + zl], place)
            running = push + decay * running
            total = [a + b for a, b in zip(total, logs)]
        runs.append(running)
        totals.append(total)
    return jnp.concatenate(runs + [packed_of(totals, place)], axis=0).astype(BF16)


def ends_of(near, far, place, mine):
    ends = [None] * NEAR
    every = [far[zh].astype(F32) for zh in range(FAR)]
    running = jnp.zeros((OWN, WIDTH), F32)
    for y in (3, 2, 1, 0):
        entering = jnp.zeros((OWN, WIDTH), F32)
        for zh in range(FAR - 1, -1, -1):
            entering = jnp.where(mine == zh, running, entering)
            at = 4 * OWN + 2 * y
            logs = every[zh][at : at + 1] + every[zh][at + 1 : at + 2]
            decay = decays_of([logs] * HEADS, place, APART)
            running = every[zh][y * OWN : (y + 1) * OWN] + decay * running
        for zl in (3, 2, 1, 0):
            ends[y * 4 + zl] = entering.astype(BF16)
            push, decay, _ = run_of(near[y * 4 + zl], place)
            entering = push + decay * entering
    return ends


def local_of(queries, key_rows, values, log_gates, grad_output, start):
    q, k = queries.astype(F32), key_rows.astype(F32)
    lower = ordered(STRETCH, lambda r, c: r >= c)
    stretches = []
    for n in (0, 1):
        part = slice(n * STRETCH, (n + 1) * STRETCH)
        within = dot(lower.astype(F32).astype(BF16), log_gates[part])
        total = within[STRETCH - 1 : STRETCH]
        column = dot_exact(
            log_gates[part], jnp.ones((STRETCH, WIDTH), F32), 0, 0
        )
        stretches.append((part, within, total, jnp.exp(column)))
    states, pushes, tails = [start], [], []
    for part, within, total, decay in stretches:
        tail = jnp.exp(total - within)
        tails.append(tail)
        growth = dot_exact(k[part] * tail, values[part], 0, 0)
        states.append(decay * states[-1] + growth)
        pushes.append(dot_exact(q[part] * jnp.exp(within), grad_output[part], 0, 0))
    ends = [pushes[1], None]
    grad_q, grad_k, grad_v = [], [], []
    for n, (part, within, total, decay) in enumerate(stretches):
        up, down = jnp.exp(within), jnp.exp(-within)
        query_up, key_down = q[part] * up, k[part] * down
        go, v = grad_output[part], values[part]
        scores = jnp.where(lower, dot(go, v, 1, 1), 0.0)
        grad_q.append(up * (dot_exact(go, states[n], 1, 1) + dot_exact(scores, key_down)))
        grad = down * dot_exact(scores, query_up, 0, 0)
        weights = jnp.where(lower, dot_exact(query_up, key_down, 1, 1), 0.0)
        grad_value = dot_exact(weights, go, 0, 0)
        if ends[n] is not None:
            grad = grad + tails[n] * dot_exact(v, ends[n], 1, 1)
            grad_value = grad_value + dot_exact(k[part] * tails[n], ends[n])
        grad_k.append(grad)
        grad_v.append(grad_value)
    grad_q, grad_k = jnp.concatenate(grad_q, axis=0), jnp.concatenate(grad_k, axis=0)
    upper = ordered(LEN, lambda r, c: r <= c).astype(F32)
    gate = dot_exact(upper, q * grad_q - k * grad_k)
    tail = jnp.concatenate([tails[0] * jnp.exp(stretches[1][2]), tails[1]], axis=0)
    return grad_q.astype(BF16), grad_k, jnp.concatenate(grad_v, axis=0), gate, tail, states[2]


def value_of(end, key_rows, tail, grad_v):
    return (grad_v + dot_left(key_rows.astype(F32) * tail, end)).astype(BF16)


def keys_of(end, values, key_rows, tail, grad_k, gate, last):
    added = tail * dot(values, end, 1, 1)
    upper = ordered(LEN, lambda r, c: r <= c).astype(F32).astype(BF16)
    own = dot_right(jnp.ones((8, WIDTH), BF16), end.astype(F32) * last, 1, 1)[:1]
    gate = gate - dot_right(upper, key_rows.astype(F32) * added) + own
    return (grad_k + added).astype(BF16), gate.astype(BF16)


def push_kernel(queries, log_gates, grad_output, out):
    out[...] = push_of(queries[...], log_gates[...], grad_output[...])


def group_kernel(place, got, out):
    runs = group_of(got, place[0])
    for zh in range(FAR):
        out[zh] = runs


def ends_kernel(place, near, far, out):
    ends = ends_of(near, far, place[0], place[1])
    for i in range(NEAR):
        out[i] = ends[i]


def local_kernel(queries, key_rows, values, log_gates, grad_output, start, grad_q, grad_k, grad_v, gate, tail, last):
    for h in range(HEADS):
        at = slice(h * WIDTH, (h + 1) * WIDTH)
        results = local_of(
            queries[:, at], key_rows[:, at], values[:, at], log_gates[:, at], grad_output[:, at], start[0, h]
        )
        for ref, value in zip((grad_q, grad_k, grad_v, gate, tail), results):
            ref[:, at] = value
        last[h] = results[5]


def end_of(every, h):
    return every[:, 8 * h : 8 * h + 8].reshape(LEN, WIDTH).astype(BF16)


def value_kernel(ends, key_rows, tail, grad_v, inputs, before, out_v, taps, padded):
    padded[:8] = before[...].astype(F32)
    padded[8:] = inputs[...].astype(F32)
    every = ends[...].astype(F32)
    for h in range(HEADS):
        at = slice(h * WIDTH, (h + 1) * WIDTH)
        grad_value = value_of(end_of(every, h), key_rows[:, at], tail[:, at], grad_v[:, at])
        out_v[:, at] = grad_value
        rounded = grad_value.astype(F32)
        for tap in range(TAPS):
            term = jnp.sum(padded[8 - tap : 8 - tap + LEN, at] * rounded, axis=0, keepdims=True)
            taps[:, tap : tap + 1, at] = jnp.broadcast_to(term[None], (NEAR, 1, WIDTH))


def keys_kernel(ends, values, key_rows, tail, grad_k, gate, last, out_k, out_gate):
    every = ends[...].astype(F32)
    for h in range(HEADS):
        at = slice(h * WIDTH, (h + 1) * WIDTH)
        out_k[:, at], out_gate[:, at] = keys_of(
            end_of(every, h), values[:, at], key_rows[:, at], tail[:, at], grad_k[:, at], gate[:, at], last[h]
        )


def conv_kernel_body(place, grad_v, after, weights, mine, other, padded, rows):
    padded[:LEN] = grad_v[...].astype(F32)
    padded[LEN:] = after[...].astype(F32)
    total = weights[0:1] * padded[0:LEN]
    for tap in range(1, TAPS):
        total = total + weights[tap : tap + 1] * padded[tap : tap + LEN]
    rows[...] = total.reshape(PEERS, LEN // PEERS, HEADS * WIDTH)
    for r in range(PEERS // 2):
        mine[r] = rows[place[2] ^ (2 * r)].astype(BF16)
        other[r] = rows[place[2] ^ (2 * r + 1)].astype(BF16)


def pack_kernel(mine, other, *outs):
    for r in range(1, PEERS // 2):
        outs[r - 1][0] = mine[r]
        outs[r - 1][1] = other[r]


def join_kernel(place, mine, other, *refs):
    out = refs[PEERS // 2 - 1]
    for r in range(PEERS // 2):
        for core in (0, 1):
            if r:
                piece = refs[r - 1][core]
            else:
                piece = (mine, other)[core][0]
            start = pl.multiple_of((place[2] ^ (2 * r + core)) * (HEADS * WIDTH), WIDTH)
            out[:, pl.ds(start, HEADS * WIDTH)] = piece


def call(kernel, outs, scalars=0, scratch=()):
    shapes = [jax.ShapeDtypeStruct(shape, dtype) for shape, dtype in outs]
    vmem = pl.BlockSpec()

    def run(*args):
        return pl.pallas_call(
            kernel,
            out_shape=shapes,
            in_specs=[pl.BlockSpec(memory_space=pltpu.SMEM)] * scalars + [vmem] * (len(args) - scalars),
            out_specs=[vmem] * len(outs),
            scratch_shapes=list(scratch),
        )(*args)

    return run


def exchange(x, axis):
    return lax.all_to_all(x, axis, 0, 0, tiled=True)


def passed_along(x, by):
    count = lax.axis_size(SEQ)
    pairs = [(i, i + by) for i in range(count) if 0 <= i + by < count]
    return lax.ppermute(x, SEQ, pairs)


def per_device(queries, key_rows, values, conv_input, log_gates, grad_output, saved_state, conv_kernel):
    columns = HEADS * WIDTH
    wide = (LEN, columns)
    place = jnp.stack([lax.axis_index(GROUP), lax.axis_index("zh"), lax.axis_index(HEAD)]).astype(jnp.int32)
    (sent,) = call(push_kernel, [((NEAR, ROWS, WIDTH), BF16)])(queries, log_gates, grad_output)
    near = exchange(sent, GROUP)
    (sent,) = call(group_kernel, [((FAR, FAR_ROWS, WIDTH), BF16)], 1)(place, near)
    far = exchange(sent, "zh")
    locals_ = call(
        local_kernel, [(wide, BF16), (wide, F32), (wide, F32), (wide, F32), (wide, F32), ((HEADS, WIDTH, WIDTH), F32)]
    )(queries, key_rows, values, log_gates, grad_output, saved_state)
    before = passed_along(conv_input[-8:], 1)
    near, before, locals_ = lax.optimization_barrier((near, before, locals_))
    grad_queries, grad_k, grad_v, gate, tail, last = locals_
    (sent,) = call(ends_kernel, [((NEAR, OWN, WIDTH), BF16)], 1)(place, near, far)
    ends = exchange(sent, GROUP)
    weights = lax.dynamic_slice_in_dim(conv_kernel, lax.axis_index(HEAD) * columns, columns, 1)
    grad_rows, taps = call(
        value_kernel, [(wide, BF16), ((NEAR, TAPS, columns), F32)], scratch=[pltpu.VMEM((LEN + 8, columns), F32)]
    )(ends, key_rows, tail, grad_v, conv_input, before)
    grad_keys, grad_gates = call(keys_kernel, [(wide, BF16), (wide, BF16)])(
        ends, values, key_rows, tail, grad_k, gate, last
    )
    taps = jnp.sum(exchange(taps, GROUP), axis=0).astype(BF16)
    summed = exchange(jnp.broadcast_to(taps[None], (FAR, TAPS, columns)), "zh")
    after = passed_along(grad_rows[:8], -1)
    piece = (LEN // PEERS, columns)
    half = PEERS // 2
    mine, other = call(
        conv_kernel_body,
        [((half,) + piece, BF16)] * 2,
        1,
        [pltpu.VMEM((LEN + 8, columns), F32), pltpu.VMEM((PEERS,) + piece, F32)],
    )(place, grad_rows, after, weights)
    other = lax.ppermute(other, HEAD, [(i, i ^ 1) for i in range(PEERS)])
    sent = call(pack_kernel, [((2,) + piece, BF16)] * (half - 1))(mine, other)
    pieces = [
        lax.ppermute(sent[r - 1], HEAD, [(i, i ^ (2 * r)) for i in range(PEERS)]) for r in range(1, half)
    ]
    (grad_input,) = call(join_kernel, [((LEN // PEERS, PEERS * columns), BF16)], 1)(place, mine, other, *pieces)
    grad_kernel = jnp.sum(summed.astype(F32), axis=0)
    return (grad_queries, grad_keys, grad_gates, grad_input, grad_kernel)


def solution(mesh):
    fine = Mesh(mesh.devices.reshape(4, FAR, 4, 4, 2), SEQ + HEAD)
    rows = P(SEQ, HEAD)
    return jax.shard_map(
        per_device,
        mesh=fine,
        in_specs=(rows, rows, rows, rows, rows, rows, P(SEQ, HEAD, None, None), P()),
        out_specs=(rows, rows, rows, P(SEQ + HEAD, None), P(None, HEAD)),
        check_vma=False,
    )
```
